32 devices in a mesh: tile: 16 (over z, y, x), band: 2 (over core).
Axes of the slice: x: 2, y: 2, z: 4, core: 2. Of those that a mesh axis runs over, the one named last changes fastest.
Arguments:
- voxel_feat: bfloat16 [4096, 64, 256], P(('tile', 'band')), may hold values from -6 to 6
- window_count: int32 [4096], P(('tile', 'band')), may hold values from 1 to 64
- voxel_cell: int32 [4096, 64], P(('tile', 'band')), may hold values from 0 to 2047
- w_qkv_voxel: bfloat16 [256, 768], replicated, may hold values from -1 to 1
- w_out_voxel: bfloat16 [256, 256], replicated, may hold values from -0.375 to 0.375
- w_up_voxel: bfloat16 [256, 512], replicated, may hold values from -0.375 to 0.375
- w_down_voxel: bfloat16 [512, 256], replicated, may hold values from -0.25 to 0.25
- conv_taps: float32 [9, 256], replicated, may hold values from -2 to 2
- w_qkv_bev: bfloat16 [256, 768], replicated, may hold values from -1 to 1
- w_out_bev: bfloat16 [256, 256], replicated, may hold values from -0.375 to 0.375
- w_up_bev: bfloat16 [256, 512], replicated, may hold values from -0.375 to 0.375
- w_down_bev: bfloat16 [512, 256], replicated, may hold values from -0.25 to 0.25
Outputs:
- bev_out: bfloat16 [256, 128, 256], P(('tile', 'band'))
The draws below stay inside these ranges and needn't reach their ends.
Inputs may be any that keep to these rules, and one draw needn't show every extreme that they name: The live slots of a window are its first window_count slots. `voxel_cell`: read only for live slots.
All inputs are finite; a program needn't handle non-finite values.
Results may differ from the reference program's by a relative error of at most 0.035.
Values may be sent and summed in bfloat16 or wider, within the bound.
A program may use at most 192 MiB of HBM per device.

```python
import jax
import jax.numpy as jnp
from jax import lax

D = 256
HEADS = 8
FF = 512
SLOT = 64
WSIDE = 8
WIN = 128
CB = 8
WINDOWS = 4096
TILE_CELLS = 2048
N_TILE = 16
N_BAND = 2


def projection_matrix(key):
    entries = jax.random.normal(key, (D, 3 * D), jnp.float32) * D ** (-0.5)
    entries = jnp.clip(entries, -6.0 * D ** (-0.5), 6.0 * D ** (-0.5))
    return entries.astype(jnp.bfloat16)


def draw_w_qkv_voxel(key, part):
    return projection_matrix(jax.random.fold_in(key, 101))


def draw_w_qkv_bev(key, part):
    return projection_matrix(jax.random.fold_in(key, 202))


def set_ends(array, key, low, largest):
    place = [jax.random.randint(jax.random.fold_in(key, axis), (), 0, length) for axis, length in enumerate(array.shape)]
    widest = array.shape.index(max(array.shape))
    neighbour = place[:widest] + [(place[widest] + 1) % array.shape[widest]] + place[widest + 1:]
    return array.at[tuple(place)].set(low).at[tuple(neighbour)].set(largest)


def block_levels(stream_key, shape, shards, smallest, high):
    def one(dim, parts):
        steps = jax.random.uniform(jax.random.fold_in(jax.random.fold_in(stream_key, 6), dim), (parts,), jnp.float32, smallest / len(shards), high / len(shards))
        return jnp.repeat(jnp.exp(steps), shape[dim] // parts).reshape((-1,) + (1,) * (len(shape) - dim - 1))

    factor_of = one(*shards[0])
    for cut in shards[1:]:
        factor_of = factor_of * one(*cut)
    return factor_of


def noise(own_key, dims, deviation, reach, shards=(), kind=jnp.bfloat16):
    values = jax.random.normal(own_key, dims, jnp.float32) * deviation
    if len(shards) > 0:
        values = block_levels(own_key, dims, shards, -0.22, 0.18) * values
    return jnp.clip(values, min=-reach, max=reach).astype(kind)


def setup_inputs(seed: int = 0) -> dict:
    key_list = jax.random.split(jax.random.key(seed), 13)
    return {
        "voxel_feat": noise(key_list[0], (WINDOWS, SLOT, D), 1.0, 6.0, ((0, 32),)),
        "window_count": set_ends(jax.random.randint(key_list[1], (WINDOWS,), 1, SLOT + 1), jax.random.fold_in(key_list[1], 1), 1, SLOT).astype(jnp.int32),
        "voxel_cell": set_ends(jax.random.randint(key_list[2], (WINDOWS, SLOT), 0, TILE_CELLS), jax.random.fold_in(key_list[2], 1), 0, TILE_CELLS - 1).astype(jnp.int32),
        "w_qkv_voxel": draw_w_qkv_voxel(jax.random.fold_in(key_list[12], 71), 0),
        "w_out_voxel": noise(key_list[4], (D, D), D ** -0.5, 0.375),
        "w_up_voxel": noise(key_list[5], (D, FF), D ** -0.5, 0.375),
        "w_down_voxel": noise(key_list[6], (FF, D), FF ** -0.5, 0.25),
        "conv_taps": noise(key_list[7], (9, D), 9 ** -0.5, 2.0, (), jnp.float32),
        "w_qkv_bev": draw_w_qkv_bev(jax.random.fold_in(key_list[12], 71), 0),
        "w_out_bev": noise(key_list[9], (D, D), D ** -0.5, 0.375),
        "w_up_bev": noise(key_list[10], (D, FF), D ** -0.5, 0.375),
        "w_down_bev": noise(key_list[11], (FF, D), FF ** -0.5, 0.25),
    }


def layer_norm(values):
    center = values - lax.optimization_barrier(jnp.mean(values, axis=-1, keepdims=True))
    spread = lax.optimization_barrier(jnp.mean(center * center, axis=-1, keepdims=True))
    return center * lax.rsqrt(spread + 1e-05)

def attend_block(windows, keep, w_qkv, w_out, w_up, w_down):
    groups, slots, width = windows.shape
    head_dim = width // HEADS
    packed = jnp.einsum('gsd,de->gse', windows.astype(jnp.float32), w_qkv.astype(jnp.float32)).astype(jnp.bfloat16)
    queries = packed[:, :, :width].reshape(groups, slots, HEADS, head_dim)
    keys_part = packed[:, :, width:2 * width].reshape(groups, slots, HEADS, head_dim)
    vals_part = packed[:, :, 2 * width:].reshape(groups, slots, HEADS, head_dim)
    scores = jnp.einsum('gqhe,gkhe->ghqk', queries.astype(jnp.float32), keys_part.astype(jnp.float32)) * head_dim ** (-0.5)
    if keep is not None:
        scores = jnp.where(keep[:, None, None, :], scores, -1e+30)
    top = lax.optimization_barrier(jnp.max(scores, axis=-1, keepdims=True))
    raised = jnp.exp(scores - top)
    weights = (raised / lax.optimization_barrier(jnp.sum(raised, axis=-1, keepdims=True))).astype(jnp.bfloat16)
    mixed = jnp.einsum('ghqk,gkhe->gqhe', weights.astype(jnp.float32), vals_part.astype(jnp.float32)).astype(jnp.bfloat16)
    mixed = mixed.reshape(groups, slots, width)
    projected = jnp.einsum('gsd,de->gse', mixed.astype(jnp.float32), w_out.astype(jnp.float32))
    hidden = layer_norm(windows.astype(jnp.float32) + projected).astype(jnp.bfloat16)
    lifted = jax.nn.relu(jnp.einsum('gsd,de->gse', hidden.astype(jnp.float32), w_up.astype(jnp.float32))).astype(jnp.bfloat16)
    lowered = jnp.einsum('gsf,fd->gsd', lifted.astype(jnp.float32), w_down.astype(jnp.float32))
    return layer_norm(hidden.astype(jnp.float32) + lowered).astype(jnp.bfloat16)

def reference(voxel_feat, window_count, voxel_cell, w_qkv_voxel, w_out_voxel, w_up_voxel, w_down_voxel, conv_taps, w_qkv_bev, w_out_bev, w_up_bev, w_down_bev):
    n_groups = N_TILE * N_BAND
    rows = WSIDE * n_groups
    cols = CB * N_TILE
    slot_ids = jnp.arange(SLOT, dtype=jnp.int32)
    keep_all = slot_ids[None, :] < window_count[:, None]
    grouped = voxel_feat.reshape(n_groups, WIN, SLOT, D)
    keep_grouped = keep_all.reshape(n_groups, WIN, SLOT)

    def first_section(pair):
        return attend_block(pair[0], pair[1], w_qkv_voxel, w_out_voxel, w_up_voxel, w_down_voxel)
    encoded = lax.map(first_section, (grouped, keep_grouped)).reshape(n_groups * WIN, SLOT, D)
    window_ids = jnp.arange(n_groups * WIN, dtype=jnp.int32)
    group_of = window_ids // WIN
    tile_of = group_of // N_BAND
    band_of = group_of % N_BAND
    cell_row = voxel_cell // CB
    cell_col = voxel_cell % CB + tile_of[:, None] * CB
    target = band_of[:, None] * (rows * cols) + cell_row * cols + cell_col
    target = jnp.where(keep_all, target, N_BAND * rows * cols).astype(jnp.int32)
    pooled = jax.ops.segment_sum(encoded.reshape(-1, D).astype(jnp.float32), target.reshape(-1), num_segments=N_BAND * rows * cols + 1)
    per_band = pooled[:-1].astype(jnp.bfloat16).reshape(N_BAND, rows, cols, D)
    total = per_band[0].astype(jnp.float32) + per_band[1].astype(jnp.float32)
    bev = layer_norm(total).astype(jnp.bfloat16)
    padded = jnp.pad(bev, ((1, 1), (1, 1), (0, 0)))
    position = jnp.zeros((rows, cols, D), jnp.float32)
    for row_tap in range(3):
        for col_tap in range(3):
            position = position + padded[row_tap:row_tap + rows, col_tap:col_tap + cols].astype(jnp.float32) * conv_taps[3 * row_tap + col_tap].astype(jnp.float32)
    shaped = (bev.astype(jnp.float32) + position).astype(jnp.bfloat16)
    across = cols // WSIDE
    windows = shaped.reshape(n_groups, WSIDE, across, WSIDE, D).transpose(0, 2, 1, 3, 4).reshape(n_groups, across, WSIDE * WSIDE, D)

    def second_section(strip):
        return attend_block(strip, None, w_qkv_bev, w_out_bev, w_up_bev, w_down_bev)
    result = lax.map(second_section, windows)
    result = result.reshape(n_groups, across, WSIDE, WSIDE, D).transpose(0, 2, 1, 3, 4).reshape(rows, cols, D)
    return result
```

```python
import functools
import math

import jax
import jax.numpy as jnp
from jax import lax
from jax.experimental import pallas as pl
from jax.experimental.pallas import tpu as pltpu
from jax.sharding import PartitionSpec as P

HEADS = 8
WSIDE = 8
CB = 8
LANES = 128
CHUNK = 8
GROUP = 4


def layer_norm(values, axis=-1):
    center = values - jnp.mean(values, axis=axis, keepdims=True)
    spread = jnp.mean(center * center, axis=axis, keepdims=True)
    return center * lax.rsqrt(spread + 1e-05)


def dot(a, b, contract=(1, 0)):
    return lax.dot_general(
        a, b, (((contract[0],), (contract[1],)), ((), ())), preferred_element_type=jnp.float32
    )


class Mixer:
    def __init__(self, tokens, width, bias_of=None):
        self.tokens, self.width, self.bias_of = tokens, width, bias_of
        self.head_dim = width // HEADS
        self.heads = LANES // self.head_dim
        self.slots = LANES // 2
        lane = lax.broadcasted_iota(jnp.int32, (LANES, LANES), 1)
        row = lax.broadcasted_iota(jnp.int32, (LANES, LANES), 0)
        self.first = (lane < self.slots).astype(jnp.bfloat16)
        self.second = 1 - self.first
        key_head = lane[: self.slots] // self.head_dim
        self.key_masks = [(key_head == h).astype(jnp.bfloat16) for h in range(self.heads)]
        self.val_masks = [
            (row // self.head_dim == h).astype(jnp.bfloat16) for h in range(self.heads)
        ]
        self.units = [
            (pair, half) for pair in range(tokens // LANES) for half in range(width // LANES)
        ]
        self.scored = {}
        self.parts = {}
        self.biases = {}

    def turn(self, x, w_qv):
        turned = dot(w_qv, x, (1, 1))
        self.queries = turned[: self.width].astype(jnp.bfloat16)
        self.vals = turned[self.width :].astype(jnp.bfloat16)

    def key(self, x, w_k):
        self.keys = dot(x, w_k).astype(jnp.bfloat16)

    def score(self, unit):
        pair, half = unit
        at, f, slots = pair * LANES, half * LANES, self.slots
        q = self.queries[f : f + LANES, at : at + LANES]
        q_blocks = jnp.concatenate([q * self.first, q * self.second], axis=0)
        sides = []
        for w in range(2):
            k = self.keys[at + w * slots : at + (w + 1) * slots, f : f + LANES]
            sides.append(jnp.concatenate([k * m for m in self.key_masks], axis=0))
        k_blocks = jnp.concatenate(sides, axis=1)
        scores = dot(k_blocks, q_blocks).reshape(self.heads, slots, LANES)
        if self.bias_of is not None:
            if pair not in self.biases:
                self.biases[pair] = self.bias_of(pair)
            scores = scores + self.biases[pair][None]
        self.scored[unit] = scores

    def mix(self, unit):
        pair, half = unit
        at, f, slots = pair * LANES, half * LANES, self.slots
        factor = self.head_dim ** (-0.5) * math.log2(math.e)
        scores = self.scored.pop(unit)
        top = jnp.max(scores, axis=1, keepdims=True)
        raised = jnp.exp2((scores - top) * factor)
        total = jnp.sum(raised, axis=1, keepdims=True)
        weights = raised.astype(jnp.bfloat16)
        v = self.vals[f : f + LANES, at : at + LANES]
        v_blocks = jnp.concatenate([v * m for m in self.val_masks], axis=1)
        spread = jnp.concatenate(
            [
                weights[h] * m
                for h in range(self.heads)
                for m in (self.first[:slots], self.second[:slots])
            ],
            axis=0,
        )
        out = dot(v_blocks, spread)
        out = out.reshape(self.heads, self.head_dim, LANES) / total
        self.parts[unit] = out.reshape(LANES, LANES).astype(jnp.bfloat16)

    def mixed(self):
        pairs, halves = self.tokens // LANES, self.width // LANES
        return jnp.concatenate(
            [
                jnp.concatenate([self.parts[p, h] for h in range(halves)], axis=0)
                for p in range(pairs)
            ],
            axis=1,
        )


def attend_columns(x, w_qv, w_k, w_out, w_up, w_down):
    mixer = Mixer(x.shape[0], x.shape[1])
    mixer.turn(x, w_qv)
    mixer.key(x, w_k)
    for unit in mixer.units:
        mixer.score(unit)
        mixer.mix(unit)
    projected = dot(w_out, mixer.mixed())
    hidden = layer_norm(x.astype(jnp.float32).T + projected, 0).astype(jnp.bfloat16)
    lifted = jax.nn.relu(dot(w_up, hidden)).astype(jnp.bfloat16)
    lowered = dot(w_down, lifted)
    return layer_norm(hidden.astype(jnp.float32) + lowered, 0)


def turn_weights(qkv_ref, out_ref, up_ref, down_ref, qv_s, out_s, up_s, down_s):
    width = out_ref.shape[0]

    def turned(values):
        return values.astype(jnp.float32).T.astype(jnp.bfloat16)

    qv_s[:width, :] = turned(qkv_ref[:, :width])
    qv_s[width:, :] = turned(qkv_ref[:, 2 * width :])
    out_s[...] = turned(out_ref[...])
    up_s[...] = turned(up_ref[...])
    down_s[...] = turned(down_ref[...])


def turned_scratch(w_qkv, w_out, w_up, w_down):
    width = w_out.shape[0]
    return [
        pltpu.VMEM((2 * width, width), jnp.bfloat16),
        pltpu.VMEM(w_out.shape[::-1], jnp.bfloat16),
        pltpu.VMEM(w_up.shape[::-1], jnp.bfloat16),
        pltpu.VMEM(w_down.shape[::-1], jnp.bfloat16),
    ]


def whole(array):
    return pl.BlockSpec(array.shape, lambda *_: (0,) * array.ndim)


def bin_table(counts, slots):
    windows = counts.shape[1]
    chunks = slots // CHUNK
    lanes = 2 * windows
    units = (counts + (CHUNK - 1)) // CHUNK
    wide = lax.broadcasted_iota(jnp.int32, (windows, windows), 1)
    key = jnp.broadcast_to(units * windows, (windows, windows)) + wide
    key = key.astype(jnp.float32)
    key_t = key.T
    rank = jnp.sum(jnp.where(key < key_t, 1.0, 0.0), axis=1, keepdims=True).astype(jnp.int32)
    count_t = jnp.broadcast_to(counts, (windows, windows)).astype(jnp.float32).T[:, :1]
    alone = jnp.zeros((1, 1), jnp.int32)
    for large in range(chunks // 2 + 1, chunks + 1):
        many = jnp.sum(jnp.where(units >= large, 1, 0), axis=1, keepdims=True)
        few = jnp.sum(jnp.where(units <= chunks - large, 1, 0), axis=1, keepdims=True)
        alone = jnp.maximum(alone, many - few)
    rest = windows - alone
    pairs = (rest + 1) // 2
    lane = lax.broadcasted_iota(jnp.int32, (1, lanes), 1)
    paired = lane < pairs
    rank_a = jnp.where(paired, lane, rest + lane - pairs)
    rank_b = jnp.where(paired, rest - 1 - lane, rank_a)
    index = lax.broadcasted_iota(jnp.int32, (windows, 1), 0).astype(jnp.float32)

    def pick(ranks, values):
        return jnp.sum(jnp.where(rank == ranks, values, 0.0), axis=0, keepdims=True).astype(jnp.int32)

    win_a, win_b = pick(rank_a, index), pick(rank_b, index)
    count_a, count_b = pick(rank_a, count_t), pick(rank_b, count_t)
    single = rank_a == rank_b
    size_a = jnp.where(single, chunks // 2, (count_a + (CHUNK - 1)) // CHUNK)
    source_b = jnp.where(single, win_a * chunks + chunks // 2, win_b * chunks)
    split = jnp.where(single, slots, size_a * CHUNK)
    end_b = jnp.where(single, 0, split + count_b)
    bins = jnp.broadcast_to(pairs + alone, (1, lanes))
    return jnp.concatenate([win_a, size_a, source_b, win_b, split, count_a, end_b, bins], axis=0)


def voxel_kernel(
    count_ref,
    x_hbm,
    cell_ref,
    qkv_ref,
    out_ref,
    up_ref,
    down_ref,
    pooled_ref,
    acc,
    xbuf,
    table_v,
    table,
    twice,
    mixed_s,
    turned_s,
    target_s,
    rows_s,
    qv_s,
    out_s,
    up_s,
    down_s,
    x_sem,
    table_sem,
):
    width = out_ref.shape[0]
    slots = cell_ref.shape[1]
    chunks = slots // CHUNK
    span = GROUP * slots
    cells = acc.shape[0]
    block = rows_s.shape[0]

    table_v[...] = bin_table(count_ref[...], slots)
    to_table = pltpu.make_async_copy(table_v, table, table_sem)
    to_table.start()
    turn_weights(qkv_ref, out_ref, up_ref, down_ref, qv_s, out_s, up_s, down_s)
    twice[...] = jnp.concatenate([cell_ref[...], cell_ref[...]], axis=1)
    to_table.wait()
    groups = (table[7, 0] + (GROUP - 1)) // GROUP

    def fetch(g, slot):
        for k in range(GROUP):
            b = g * GROUP + k
            size = table[1, b]
            at = k * chunks
            pltpu.make_async_copy(
                x_hbm.at[pl.ds(table[0, b] * chunks, size)],
                xbuf.at[slot, pl.ds(at, size)],
                x_sem.at[slot],
            ).start()
            pltpu.make_async_copy(
                x_hbm.at[pl.ds(table[2, b], chunks - size)],
                xbuf.at[slot, pl.ds(at + size, chunks - size)],
                x_sem.at[slot],
            ).start()

    def fetched(slot):
        pltpu.make_async_copy(
            x_hbm.at[pl.ds(0, GROUP * chunks)], xbuf.at[slot], x_sem.at[slot]
        ).wait()

    fetch(0, 0)
    acc[...] = jnp.zeros_like(acc)
    mixed_s[...] = jnp.zeros_like(mixed_s)
    turned_s[...] = jnp.zeros_like(turned_s)
    target_s[...] = jnp.full_like(target_s, -1.0)
    rows_s[...] = lax.broadcasted_iota(jnp.int32, rows_s.shape, 0).astype(jnp.float32).astype(jnp.bfloat16)

    lane = lax.broadcasted_iota(jnp.int32, (1, LANES), 1)
    first = lane < slots
    place = lane % slots
    key_row = lax.broadcasted_iota(jnp.int32, (slots, LANES), 0)

    def limits_of(g):
        limits = []
        targets = []
        for pair in range(span // LANES):
            pick = []
            for half in range(2):
                b = g * GROUP + 2 * pair + half
                split = table[4, b]
                own = twice[pl.ds(table[0, b], 1), :]
                other = twice[pl.ds(table[3, b], 1), :]
                other = pltpu.roll(other, lax.rem(split, slots), 1)
                pick.append(
                    (split, table[5, b], table[6, b], jnp.where(place < split, own, other))
                )
            split, count, end, cell = [jnp.where(first, u, v) for u, v in zip(*pick)]
            late = place >= split
            low = jnp.where(late, split, 0)
            high = jnp.where(late, end, count)
            limits.append((low, high))
            live = jnp.logical_and(place >= low, place < high)
            targets.append(jnp.where(live, cell, -1).astype(jnp.float32))
        return limits, jnp.concatenate(targets, axis=1)

    def step(g, carry):
        slot = lax.rem(g, 2)
        fetch(g + 1, 1 - slot)
        fetched(slot)
        limits, next_target = limits_of(g)

        def bias_of(pair):
            low, high = limits[pair]
            return jnp.where(jnp.logical_and(key_row >= low, key_row < high), 0.0, -1e30)

        mixer = Mixer(span, width, bias_of)
        target = target_s[...]
        one, none = jnp.bfloat16(1), jnp.bfloat16(0)

        def pool(c):
            near = (target - float(c * block)).astype(jnp.bfloat16)
            hot = jnp.where(rows_s[...] == near, one, none)
            at = slice(c * block, (c + 1) * block)
            acc[at, :] += dot(hot, encoded)

        x = xbuf[slot].astype(jnp.float32).reshape(span, width)
        x_b = x.astype(jnp.bfloat16)
        units = mixer.units
        mixer.turn(x_b, qv_s[...])
        projected = dot(out_s[...], mixed_s[...])
        mixer.key(x_b, qkv_ref[:, width : 2 * width])
        mixer.score(units[0])
        hidden = layer_norm(turned_s[...].astype(jnp.float32) + projected, 0).astype(jnp.bfloat16)
        turned_s[...] = x.T.astype(jnp.bfloat16)
        lifted = jax.nn.relu(dot(up_s[...], hidden)).astype(jnp.bfloat16)
        mixer.score(units[1])
        mixer.mix(units[0])
        lowered = dot(down_s[...], lifted)
        mixer.score(units[2])
        mixer.mix(units[1])
        encoded = layer_norm(hidden.astype(jnp.float32) + lowered, 0).T.astype(jnp.bfloat16)
        mixer.score(units[3])
        mixer.mix(units[2])
        blocks = cells // block
        for c in range(blocks // 2):
            pool(c)
        mixer.mix(units[3])
        for c in range(blocks // 2, blocks):
            pool(c)
        target_s[...] = next_target
        mixed_s[...] = mixer.mixed()
        return carry

    lax.fori_loop(0, groups + 1, step, 0)
    fetched(lax.rem(groups + 1, 2))
    pooled_ref[...] = acc[...].astype(jnp.bfloat16)


def voxel_pool(feat, counts, cell, weights, cells):
    windows, slots, width = feat.shape
    vmem = pl.BlockSpec(memory_space=pltpu.VMEM)
    span = GROUP * slots
    chunks = slots // CHUNK
    block = math.gcd(cells, 256)
    return pl.pallas_call(
        voxel_kernel,
        in_specs=[vmem, pl.BlockSpec(memory_space=pl.ANY)] + [vmem] * 5,
        out_specs=vmem,
        out_shape=jax.ShapeDtypeStruct((cells, width), jnp.bfloat16),
        scratch_shapes=[
            pltpu.VMEM((cells, width), jnp.float32),
            pltpu.VMEM((2, GROUP * chunks, CHUNK, width), jnp.bfloat16),
            pltpu.VMEM((8, 2 * windows), jnp.int32),
            pltpu.SMEM((8, 2 * windows), jnp.int32),
            pltpu.VMEM((windows, 2 * slots), jnp.int32),
            pltpu.VMEM((width, span), jnp.bfloat16),
            pltpu.VMEM((width, span), jnp.bfloat16),
            pltpu.VMEM((1, span), jnp.float32),
            pltpu.VMEM((block, span), jnp.bfloat16),
        ]
        + turned_scratch(*weights)
        + [pltpu.SemaphoreType.DMA((2,)), pltpu.SemaphoreType.DMA],
        name="voxel_pool",
    )(
        counts.reshape(1, windows),
        feat.reshape(windows * chunks, CHUNK, width),
        cell,
        *weights,
    )


def pool_kernel(
    n_tile,
    n_band,
    pooled_ref,
    grid_ref,
    low_ref,
    high_ref,
    came,
    ready,
    landed,
    low,
    high,
    swap_send,
    swap_recv,
    send,
    recv,
    halo_send,
    halo_recv,
):
    tile = lax.axis_index("tile")
    band = lax.axis_index("band")
    other = 1 - band
    strip = tile * n_band + band
    width = pooled_ref.shape[3]
    blocks = came.shape[0]
    per = n_tile // blocks
    cells = WSIDE * CB
    mesh_id = pl.DeviceIdType.MESH

    def strip_id(s):
        return (s // n_band, s % n_band)

    barrier = pltpu.get_barrier_semaphore()

    def greet(i, carry):
        peer = lax.rem(tile + i, n_tile)
        pl.semaphore_signal(barrier, inc=1, device_id=(peer, band), device_id_type=mesh_id)
        return carry

    lax.fori_loop(1, n_tile, greet, 0)
    pl.semaphore_signal(barrier, inc=1, device_id=(tile, other), device_id_type=mesh_id)
    across_below = jnp.logical_and(band == 0, tile > 0)
    across_above = jnp.logical_and(band == n_band - 1, tile < n_tile - 1)

    @pl.when(across_below)
    def _():
        pl.semaphore_signal(barrier, inc=1, device_id=strip_id(strip - 1), device_id_type=mesh_id)

    @pl.when(across_above)
    def _():
        pl.semaphore_signal(barrier, inc=1, device_id=strip_id(strip + 1), device_id_type=mesh_id)

    across = jnp.logical_or(across_below, across_above)

    @pl.when(across)
    def _():
        pl.semaphore_wait(barrier, n_tile + 1)

    @pl.when(jnp.logical_not(across))
    def _():
        pl.semaphore_wait(barrier, n_tile)

    def place(i):
        ahead = jnp.where(i < blocks - blocks // 2, blocks // 2 + i, blocks - 1 - i)
        return lax.rem(tile // per + ahead, blocks)

    def swap(j):
        return pltpu.make_async_remote_copy(
            src_ref=pooled_ref.at[pl.ds(j * per, per), other],
            dst_ref=came.at[j],
            send_sem=swap_send.at[j],
            recv_sem=swap_recv.at[j],
            device_id=(tile, other),
            device_id_type=mesh_id,
        )

    def deliver(dest, source):
        return pltpu.make_async_remote_copy(
            src_ref=ready.at[dest],
            dst_ref=landed.at[source],
            send_sem=send.at[dest],
            recv_sem=recv.at[source],
            device_id=(dest, band),
            device_id_type=mesh_id,
        )

    def finish(i):
        j = place(i)
        swap(j).wait_recv()
        mine = pooled_ref[pl.ds(j * per, per), band].astype(jnp.float32)
        total = mine + came[j].astype(jnp.float32)
        normal = layer_norm(total).reshape(per, WSIDE, CB, width).astype(jnp.bfloat16)
        for d in range(per):
            dest = j * per + d

            @pl.when(dest != tile)
            def _():
                ready[dest] = normal[d]
                deliver(dest, tile).start()

            @pl.when(dest == tile)
            def _():
                landed[tile] = normal[d]

    def swap_start(i, carry):
        swap(place(i)).start()
        return carry

    lax.fori_loop(0, blocks, swap_start, 0)

    def swap_finish(i, carry):
        finish(i)
        return carry

    lax.fori_loop(0, blocks, swap_finish, 0)

    def arrive(i, carry):
        peer = lax.rem(tile + i, n_tile)
        deliver(peer, peer).wait_recv()
        return carry

    lax.fori_loop(1, n_tile, arrive, 0)

    def edge(side, target):
        return pltpu.make_async_remote_copy(
            src_ref=landed.at[:, 0 if side == 0 else WSIDE - 1],
            dst_ref=high if side == 0 else low,
            send_sem=halo_send.at[side],
            recv_sem=halo_recv.at[side],
            device_id=strip_id(target),
            device_id_type=mesh_id,
        )

    has_below = strip > 0
    has_above = strip < n_tile * n_band - 1

    @pl.when(has_below)
    def _():
        edge(0, strip - 1).start()

    @pl.when(has_above)
    def _():
        edge(1, strip + 1).start()

    grid_ref[...] = landed[...]

    def left(i, carry):
        peer = lax.rem(tile + i, n_tile)
        deliver(peer, peer).wait_send()
        return carry

    lax.fori_loop(1, n_tile, left, 0)

    def swapped(j, carry):
        swap(j).wait_send()
        return carry

    lax.fori_loop(0, blocks, swapped, 0)

    @pl.when(has_below)
    def _():
        edge(0, strip - 1).wait_send()
        edge(1, strip - 1).wait_recv()
        low_ref[...] = low[...]

    @pl.when(has_above)
    def _():
        edge(1, strip + 1).wait_send()
        edge(0, strip + 1).wait_recv()
        high_ref[...] = high[...]

    @pl.when(strip == 0)
    def _():
        low_ref[...] = jnp.zeros_like(low_ref)

    @pl.when(strip == n_tile * n_band - 1)
    def _():
        high_ref[...] = jnp.zeros_like(high_ref)


def pool_exchange(pooled, n_tile, n_band):
    cells, width = pooled.shape
    cells = WSIDE * CB
    per = math.gcd(n_tile, 4)
    blocks = n_tile // per
    half = jnp.bfloat16
    vmem = pl.BlockSpec(memory_space=pltpu.VMEM)
    return pl.pallas_call(
        functools.partial(pool_kernel, n_tile, n_band),
        in_specs=[vmem],
        out_specs=[vmem] * 3,
        out_shape=[
            jax.ShapeDtypeStruct((n_tile, WSIDE, CB, width), half),
            jax.ShapeDtypeStruct((n_tile, CB, width), half),
            jax.ShapeDtypeStruct((n_tile, CB, width), half),
        ],
        scratch_shapes=[
            pltpu.VMEM((blocks, per, cells, width), half),
            pltpu.VMEM((n_tile, WSIDE, CB, width), half),
            pltpu.VMEM((n_tile, WSIDE, CB, width), half),
            pltpu.VMEM((n_tile, CB, width), half),
            pltpu.VMEM((n_tile, CB, width), half),
            pltpu.SemaphoreType.DMA((blocks,)),
            pltpu.SemaphoreType.DMA((blocks,)),
            pltpu.SemaphoreType.DMA((n_tile,)),
            pltpu.SemaphoreType.DMA((n_tile,)),
            pltpu.SemaphoreType.DMA((2,)),
            pltpu.SemaphoreType.DMA((2,)),
        ],
        compiler_params=pltpu.CompilerParams(collective_id=0, has_side_effects=True),
        name="pool_exchange",
    )(pooled.reshape(n_tile, n_band, cells, width))


def bev_kernel(
    grid_ref,
    low_ref,
    high_ref,
    tap_ref,
    qkv_ref,
    out_ref,
    up_ref,
    down_ref,
    result_ref,
    wide,
    qv_s,
    out_s,
    up_s,
    down_s,
):
    step = pl.program_id(0)
    n_tile, _, _, width = grid_ref.shape
    span = result_ref.shape[1]

    @pl.when(step == 0)
    def _():
        turn_weights(qkv_ref, out_ref, up_ref, down_ref, qv_s, out_s, up_s, down_s)
        edge = jnp.zeros((WSIDE + 2, CB, width), jnp.float32)
        wide[:, :CB, :] = edge
        wide[:, (n_tile + 1) * CB :, :] = edge

        def fill(t, carry):
            to = pl.ds(pl.multiple_of((t + 1) * CB, CB), CB)
            wide[0, to, :] = low_ref[t].astype(jnp.float32)
            wide[WSIDE + 1, to, :] = high_ref[t].astype(jnp.float32)
            wide[1 : WSIDE + 1, to, :] = grid_ref[t].astype(jnp.float32)
            return carry

        lax.fori_loop(0, n_tile, fill, 0)

    at = pl.multiple_of(step * span, span)
    sums = [jnp.zeros((span, width), jnp.float32) for _ in range(WSIDE)]
    centers = []
    for r in range(WSIDE + 2):
        slab = wide[r, pl.ds(at, span + 2 * CB), :]
        for c in range(3):
            moved = slab[CB + c - 1 : CB + c - 1 + span]
            if c == 1:
                centers.append(moved)
            for row_tap in range(3):
                to = r - row_tap
                if 0 <= to < WSIDE:
                    tap = tap_ref[3 * row_tap + c : 3 * row_tap + c + 1, :]
                    sums[to] = sums[to] + moved * tap
    shaped = [centers[r + 1] + sums[r] for r in range(WSIDE)]
    count = span // CB
    x = jnp.concatenate(
        [shaped[r][w * CB : (w + 1) * CB] for w in range(count) for r in range(WSIDE)], axis=0
    ).astype(jnp.bfloat16)
    result = attend_columns(
        x, qv_s[...], qkv_ref[:, width : 2 * width], out_s[...], up_s[...], down_s[...]
    ).T
    for r in range(WSIDE):
        result_ref[r] = jnp.concatenate(
            [result[(w * WSIDE + r) * CB : (w * WSIDE + r + 1) * CB] for w in range(count)], axis=0
        ).astype(jnp.bfloat16)


def bev_block(grid, low, high, taps, weights):
    n_tile, _, _, width = grid.shape
    cols = n_tile * CB
    span = min(64, cols)
    inputs = (grid, low, high, taps, *weights)
    return pl.pallas_call(
        bev_kernel,
        grid=(cols // span,),
        in_specs=[whole(a) for a in inputs],
        out_specs=pl.BlockSpec((WSIDE, span, width), lambda i: (0, i, 0)),
        out_shape=jax.ShapeDtypeStruct((WSIDE, cols, width), jnp.bfloat16),
        scratch_shapes=[pltpu.VMEM((WSIDE + 2, cols + 2 * CB, width), jnp.float32)]
        + turned_scratch(*weights),
        name="bev_block",
    )(*inputs)


def shards(
    voxel_feat,
    window_count,
    voxel_cell,
    w_qkv_voxel,
    w_out_voxel,
    w_up_voxel,
    w_down_voxel,
    conv_taps,
    w_qkv_bev,
    w_out_bev,
    w_up_bev,
    w_down_bev,
):
    n_tile = lax.axis_size("tile")
    n_band = lax.axis_size("band")
    pooled = voxel_pool(
        voxel_feat,
        window_count,
        voxel_cell,
        (w_qkv_voxel, w_out_voxel, w_up_voxel, w_down_voxel),
        WSIDE * CB * n_tile * n_band,
    )
    grid, low, high = pool_exchange(pooled, n_tile, n_band)
    return bev_block(
        grid, low, high, conv_taps, (w_qkv_bev, w_out_bev, w_up_bev, w_down_bev)
    )


def solution(mesh):
    placed = (
        P(("tile", "band"), None, None),
        P(("tile", "band")),
        P(("tile", "band"), None),
        P(),
        P(),
        P(),
        P(),
        P(),
        P(),
        P(),
        P(),
        P(),
    )
    return jax.shard_map(
        shards,
        mesh=mesh,
        in_specs=placed,
        out_specs=P(("tile", "band"), None, None),
        check_vma=False,
    )
```

```python
import functools
import math

import jax
import jax.numpy as jnp
from jax import lax
from jax.experimental import pallas as pl
from jax.experimental.pallas import tpu as pltpu
from jax.sharding import PartitionSpec as P

HEADS = 8
WSIDE = 8
CB = 8
LANES = 128
CHUNK = 8
HEADER = 8
VMEM_LIMIT = 56 * 1024 * 1024
GROUP = 4


def layer_norm(values, axis=-1):
    center = values - jnp.mean(values, axis=axis, keepdims=True)
    spread = jnp.mean(center * center, axis=axis, keepdims=True)
    return center * lax.rsqrt(spread + 1e-05)


def dot(a, b, contract=(1, 0)):
    return lax.dot_general(
        a, b, (((contract[0],), (contract[1],)), ((), ())), preferred_element_type=jnp.float32
    )


class Mixer:
    def __init__(self, tokens, width, bias_of=None):
        self.tokens, self.width, self.bias_of = tokens, width, bias_of
        self.head_dim = width // HEADS
        self.heads = LANES // self.head_dim
        self.slots = LANES // 2
        lane = lax.broadcasted_iota(jnp.int32, (LANES, LANES), 1)
        row = lax.broadcasted_iota(jnp.int32, (LANES, LANES), 0)
        self.first = (lane < self.slots).astype(jnp.bfloat16)
        self.second = 1 - self.first
        key_head = lane[: self.slots] // self.head_dim
        self.key_masks = [(key_head == h).astype(jnp.bfloat16) for h in range(self.heads)]
        self.val_masks = [
            (row // self.head_dim == h).astype(jnp.bfloat16) for h in range(self.heads)
        ]
        self.units = [
            (pair, half) for pair in range(tokens // LANES) for half in range(width // LANES)
        ]
        self.scored = {}
        self.parts = {}
        self.biases = {}

    def turn(self, x, w_qv):
        turned = dot(w_qv, x, (1, 1))
        self.queries = turned[: self.width].astype(jnp.bfloat16)
        self.vals = turned[self.width :].astype(jnp.bfloat16)

    def key(self, x, w_k):
        self.keys = dot(x, w_k).astype(jnp.bfloat16)

    def score(self, unit):
        pair, half = unit
        at, f, slots = pair * LANES, half * LANES, self.slots
        q = self.queries[f : f + LANES, at : at + LANES]
        q_blocks = jnp.concatenate([q * self.first, q * self.second], axis=0)
        sides = []
        for w in range(2):
            k = self.keys[at + w * slots : at + (w + 1) * slots, f : f + LANES]
            sides.append(jnp.concatenate([k * m for m in self.key_masks], axis=0))
        k_blocks = jnp.concatenate(sides, axis=1)
        scores = dot(k_blocks, q_blocks).reshape(self.heads, slots, LANES)
        if self.bias_of is not None:
            if pair not in self.biases:
                self.biases[pair] = self.bias_of(pair)
            scores = scores + self.biases[pair][None]
        self.scored[unit] = scores

    def mix(self, unit):
        pair, half = unit
        at, f, slots = pair * LANES, half * LANES, self.slots
        factor = self.head_dim ** (-0.5) * math.log2(math.e)
        scores = self.scored.pop(unit)
        top = jnp.max(scores, axis=1, keepdims=True)
        raised = jnp.exp2((scores - top) * factor)
        total = jnp.sum(raised, axis=1, keepdims=True)
        weights = raised.astype(jnp.bfloat16)
        v = self.vals[f : f + LANES, at : at + LANES]
        v_blocks = jnp.concatenate([v * m for m in self.val_masks], axis=1)
        spread = jnp.concatenate(
            [
                weights[h] * m
                for h in range(self.heads)
                for m in (self.first[:slots], self.second[:slots])
            ],
            axis=0,
        )
        out = dot(v_blocks, spread)
        out = out.reshape(self.heads, self.head_dim, LANES) / total
        self.parts[unit] = out.reshape(LANES, LANES).astype(jnp.bfloat16)

    def mixed(self):
        pairs, halves = self.tokens // LANES, self.width // LANES
        return jnp.concatenate(
            [
                jnp.concatenate([self.parts[p, h] for h in range(halves)], axis=0)
                for p in range(pairs)
            ],
            axis=1,
        )


def attend_columns(x, w_qv, w_k, w_out, w_up, w_down):
    mixer = Mixer(x.shape[0], x.shape[1])
    mixer.turn(x, w_qv)
    mixer.key(x, w_k)
    for unit in mixer.units:
        mixer.score(unit)
        mixer.mix(unit)
    projected = dot(w_out, mixer.mixed())
    hidden = layer_norm(x.astype(jnp.float32).T + projected, 0).astype(jnp.bfloat16)
    lifted = jax.nn.relu(dot(w_up, hidden)).astype(jnp.bfloat16)
    lowered = dot(w_down, lifted)
    return layer_norm(hidden.astype(jnp.float32) + lowered, 0)


def turn_weights(qkv_ref, out_ref, up_ref, down_ref, qv_s, out_s, up_s, down_s):
    width = out_ref.shape[0]

    def turned(values):
        return values.astype(jnp.float32).T.astype(jnp.bfloat16)

    qv_s[:width, :] = turned(qkv_ref[:, :width])
    qv_s[width:, :] = turned(qkv_ref[:, 2 * width :])
    out_s[...] = turned(out_ref[...])
    up_s[...] = turned(up_ref[...])
    down_s[...] = turned(down_ref[...])


def turned_scratch(w_qkv, w_out, w_up, w_down):
    width = w_out.shape[0]
    return [
        pltpu.VMEM((2 * width, width), jnp.bfloat16),
        pltpu.VMEM(w_out.shape[::-1], jnp.bfloat16),
        pltpu.VMEM(w_up.shape[::-1], jnp.bfloat16),
        pltpu.VMEM(w_down.shape[::-1], jnp.bfloat16),
    ]


def whole(array):
    return pl.BlockSpec(array.shape, lambda *_: (0,) * array.ndim)


def bin_table(counts, slots):
    windows = counts.shape[1]
    chunks = slots // CHUNK
    lanes = 2 * windows
    units = (counts + (CHUNK - 1)) // CHUNK
    wide = lax.broadcasted_iota(jnp.int32, (windows, windows), 1)
    key = jnp.broadcast_to(units * windows, (windows, windows)) + wide
    key = key.astype(jnp.float32)
    key_t = key.T
    rank = jnp.sum(jnp.where(key < key_t, 1.0, 0.0), axis=1, keepdims=True).astype(jnp.int32)
    count_t = jnp.broadcast_to(counts, (windows, windows)).astype(jnp.float32).T[:, :1]
    alone = jnp.zeros((1, 1), jnp.int32)
    for large in range(chunks // 2 + 1, chunks + 1):
        many = jnp.sum(jnp.where(units >= large, 1, 0), axis=1, keepdims=True)
        few = jnp.sum(jnp.where(units <= chunks - large, 1, 0), axis=1, keepdims=True)
        alone = jnp.maximum(alone, many - few)
    rest = windows - alone
    pairs = (rest + 1) // 2
    lane = lax.broadcasted_iota(jnp.int32, (1, lanes), 1)
    paired = lane < pairs
    rank_a = jnp.where(paired, lane, rest + lane - pairs)
    rank_b = jnp.where(paired, rest - 1 - lane, rank_a)
    index = lax.broadcasted_iota(jnp.int32, (windows, 1), 0).astype(jnp.float32)

    def pick(ranks, values):
        return jnp.sum(jnp.where(rank == ranks, values, 0.0), axis=0, keepdims=True).astype(jnp.int32)

    win_a, win_b = pick(rank_a, index), pick(rank_b, index)
    count_a, count_b = pick(rank_a, count_t), pick(rank_b, count_t)
    single = rank_a == rank_b
    size_a = jnp.where(single, chunks // 2, (count_a + (CHUNK - 1)) // CHUNK)
    source_b = jnp.where(single, win_a * chunks + chunks // 2, win_b * chunks)
    split = jnp.where(single, slots, size_a * CHUNK)
    end_b = jnp.where(single, 0, split + count_b)
    bins = jnp.broadcast_to(pairs + alone, (1, lanes))
    chunk = lax.broadcasted_iota(jnp.int32, (chunks, lanes), 0)
    sources = jnp.where(chunk < size_a, win_a * chunks + chunk, source_b + chunk - size_a)
    blank = jnp.zeros((HEADER - 6, lanes), jnp.int32)
    return jnp.concatenate([win_a, win_b, split, count_a, end_b, bins, blank, sources], axis=0)


def voxel_kernel(
    count_ref,
    x_hbm,
    cell_ref,
    qkv_ref,
    out_ref,
    up_ref,
    down_ref,
    pooled_ref,
    acc,
    x_s,
    table_v,
    table,
    twice,
    mixed_s,
    turned_s,
    target_s,
    older_s,
    encoded_s,
    rows_s,
    qv_s,
    out_s,
    up_s,
    down_s,
    x_sem,
    table_sem,
):
    width = out_ref.shape[0]
    slots = cell_ref.shape[0]
    chunks = slots // CHUNK
    span = GROUP * slots
    cells = acc.shape[0]
    block = rows_s.shape[0]

    load_x = pltpu.make_async_copy(x_hbm, x_s, x_sem)
    load_x.start()
    table_v[...] = bin_table(count_ref[...], slots)
    to_table = pltpu.make_async_copy(table_v, table, table_sem)
    to_table.start()
    turn_weights(qkv_ref, out_ref, up_ref, down_ref, qv_s, out_s, up_s, down_s)
    cell = cell_ref[...].astype(jnp.float32).T.astype(jnp.int32)
    twice[...] = jnp.concatenate([cell, cell], axis=1)
    to_table.wait()
    groups = (table[5, 0] + (GROUP - 1)) // GROUP

    acc[...] = jnp.zeros_like(acc)
    mixed_s[...] = jnp.zeros_like(mixed_s)
    turned_s[...] = jnp.zeros_like(turned_s)
    target_s[...] = jnp.full_like(target_s, -1.0)
    older_s[...] = jnp.full_like(older_s, -1.0)
    encoded_s[...] = jnp.zeros_like(encoded_s)
    rows_s[...] = lax.broadcasted_iota(jnp.int32, rows_s.shape, 0).astype(jnp.float32).astype(jnp.bfloat16)

    lane = lax.broadcasted_iota(jnp.int32, (1, LANES), 1)
    first = lane < slots
    place = lane % slots
    key_row = lax.broadcasted_iota(jnp.int32, (slots, LANES), 0)

    def limits_of(g):
        limits = []
        targets = []
        for pair in range(span // LANES):
            pick = []
            for half in range(2):
                b = g * GROUP + 2 * pair + half
                split = table[2, b]
                own = twice[pl.ds(table[0, b], 1), :]
                other = twice[pl.ds(table[1, b], 1), :]
                other = pltpu.roll(other, lax.rem(split, slots), 1)
                pick.append(
                    (split, table[3, b], table[4, b], jnp.where(place < split, own, other))
                )
            split, count, end, cell = [jnp.where(first, u, v) for u, v in zip(*pick)]
            late = place >= split
            low = jnp.where(late, split, 0)
            high = jnp.where(late, end, count)
            limits.append((low, high))
            live = jnp.logical_and(place >= low, place < high)
            targets.append(jnp.where(live, cell, -1).astype(jnp.float32))
        return limits, jnp.concatenate(targets, axis=1)

    blocks = cells // block

    def pool(some):
        target = older_s[...]
        encoded = encoded_s[...]
        one, none = jnp.bfloat16(1), jnp.bfloat16(0)
        for c in some:
            near = (target - float(c * block)).astype(jnp.bfloat16)
            hot = jnp.where(rows_s[...] == near, one, none)
            at = slice(c * block, (c + 1) * block)
            acc[at, :] += dot(hot, encoded)

    def step(g, carry):
        limits, next_target = limits_of(g)

        def bias_of(pair):
            low, high = limits[pair]
            return jnp.where(jnp.logical_and(key_row >= low, key_row < high), 0.0, -1e30)

        mixer = Mixer(span, width, bias_of)
        third = -(-blocks // 3)
        picks = []
        for k in range(GROUP):
            for c in range(chunks):
                picks.append(x_s[table[HEADER + c, g * GROUP + k]])
        x = jnp.concatenate([p.astype(jnp.float32) for p in picks], axis=0)
        x_b = x.astype(jnp.bfloat16)
        units = mixer.units
        projected = dot(out_s[...], mixed_s[...])
        mixer.turn(x_b, qv_s[...])
        hidden = layer_norm(turned_s[...].astype(jnp.float32) + projected, 0).astype(jnp.bfloat16)
        mixer.key(x_b, qkv_ref[:, width : 2 * width])
        turned_s[...] = x.T.astype(jnp.bfloat16)
        lifted = jax.nn.relu(dot(up_s[...], hidden)).astype(jnp.bfloat16)
        mixer.score(units[0])
        lowered = dot(down_s[...], lifted)
        mixer.score(units[1])
        mixer.mix(units[0])
        pool(range(0, third))
        encoded = layer_norm(hidden.astype(jnp.float32) + lowered, 0)
        mixer.score(units[2])
        mixer.mix(units[1])
        pool(range(third, 2 * third))
        mixer.score(units[3])
        mixer.mix(units[2])
        pool(range(2 * third, blocks))
        mixer.mix(units[3])
        target = target_s[...]
        older_s[...] = target
        target_s[...] = next_target
        encoded_s[...] = encoded.T.astype(jnp.bfloat16)
        mixed_s[...] = mixer.mixed()
        return carry

    load_x.wait()
    lax.fori_loop(0, groups + 1, step, 0)
    pool(range(blocks))
    pooled_ref[...] = acc[...].astype(jnp.bfloat16)


def voxel_pool(feat, counts, cell, weights, cells):
    windows, slots, width = feat.shape
    vmem = pl.BlockSpec(memory_space=pltpu.VMEM)
    span = GROUP * slots
    chunks = slots // CHUNK
    block = math.gcd(cells, 256)
    return pl.pallas_call(
        voxel_kernel,
        in_specs=[vmem, pl.BlockSpec(memory_space=pl.ANY)] + [vmem] * 5,
        out_specs=vmem,
        out_shape=jax.ShapeDtypeStruct((cells, width), jnp.bfloat16),
        scratch_shapes=[
            pltpu.VMEM((cells, width), jnp.float32),
            pltpu.VMEM((windows * chunks, CHUNK, width), jnp.bfloat16),
            pltpu.VMEM((HEADER + chunks, 2 * windows), jnp.int32),
            pltpu.SMEM((HEADER + chunks, 2 * windows), jnp.int32),
            pltpu.VMEM((windows, 2 * slots), jnp.int32),
            pltpu.VMEM((width, span), jnp.bfloat16),
            pltpu.VMEM((width, span), jnp.bfloat16),
            pltpu.VMEM((1, span), jnp.float32),
            pltpu.VMEM((1, span), jnp.float32),
            pltpu.VMEM((span, width), jnp.bfloat16),
            pltpu.VMEM((block, span), jnp.bfloat16),
        ]
        + turned_scratch(*weights)
        + [pltpu.SemaphoreType.DMA, pltpu.SemaphoreType.DMA],
        compiler_params=pltpu.CompilerParams(vmem_limit_bytes=VMEM_LIMIT),
        name="voxel_pool",
    )(
        counts.reshape(1, windows),
        feat.reshape(windows * chunks, CHUNK, width),
        cell.T,
        *weights,
    )


def pool_kernel(
    n_tile,
    n_band,
    pooled_ref,
    grid_ref,
    low_ref,
    high_ref,
    came,
    ready,
    landed,
    low,
    high,
    swap_send,
    swap_recv,
    send,
    recv,
    halo_send,
    halo_recv,
):
    tile = lax.axis_index("tile")
    band = lax.axis_index("band")
    other = 1 - band
    strip = tile * n_band + band
    width = pooled_ref.shape[3]
    blocks = came.shape[0]
    per = n_tile // blocks
    cells = WSIDE * CB
    mesh_id = pl.DeviceIdType.MESH

    def strip_id(s):
        return (s // n_band, s % n_band)

    barrier = pltpu.get_barrier_semaphore()

    def greet(i, carry):
        peer = lax.rem(tile + i, n_tile)
        pl.semaphore_signal(barrier, inc=1, device_id=(peer, band), device_id_type=mesh_id)
        return carry

    lax.fori_loop(1, n_tile, greet, 0)
    pl.semaphore_signal(barrier, inc=1, device_id=(tile, other), device_id_type=mesh_id)
    across_below = jnp.logical_and(band == 0, tile > 0)
    across_above = jnp.logical_and(band == n_band - 1, tile < n_tile - 1)

    @pl.when(across_below)
    def _():
        pl.semaphore_signal(barrier, inc=1, device_id=strip_id(strip - 1), device_id_type=mesh_id)

    @pl.when(across_above)
    def _():
        pl.semaphore_signal(barrier, inc=1, device_id=strip_id(strip + 1), device_id_type=mesh_id)

    across = jnp.logical_or(across_below, across_above)

    @pl.when(across)
    def _():
        pl.semaphore_wait(barrier, n_tile + 1)

    @pl.when(jnp.logical_not(across))
    def _():
        pl.semaphore_wait(barrier, n_tile)

    def place(i):
        ahead = jnp.where(i < blocks - blocks // 2, blocks // 2 + i, blocks - 1 - i)
        return lax.rem(tile // per + ahead, blocks)

    def swap(j):
        return pltpu.make_async_remote_copy(
            src_ref=pooled_ref.at[pl.ds(j * per, per), other],
            dst_ref=came.at[j],
            send_sem=swap_send.at[j],
            recv_sem=swap_recv.at[j],
            device_id=(tile, other),
            device_id_type=mesh_id,
        )

    def deliver(dest, source):
        return pltpu.make_async_remote_copy(
            src_ref=ready.at[dest],
            dst_ref=landed.at[source],
            send_sem=send.at[dest],
            recv_sem=recv.at[source],
            device_id=(dest, band),
            device_id_type=mesh_id,
        )

    def finish(i):
        j = place(i)
        swap(j).wait_recv()
        mine = pooled_ref[pl.ds(j * per, per), band].astype(jnp.float32)
        total = mine + came[j].astype(jnp.float32)
        normal = layer_norm(total).reshape(per, WSIDE, CB, width).astype(jnp.bfloat16)
        ready[pl.ds(j * per, per)] = normal
        for d in range(per):
            dest = j * per + lax.rem(tile + 1 + d, per)

            @pl.when(dest != tile)
            def _():
                deliver(dest, tile).start()

            @pl.when(dest == tile)
            def _():
                landed[tile] = ready[tile]

    def swap_start(i, carry):
        swap(place(i)).start()
        return carry

    lax.fori_loop(0, blocks, swap_start, 0)

    def swap_finish(i, carry):
        finish(i)
        return carry

    lax.fori_loop(0, blocks, swap_finish, 0)

    def arrive(i, carry):
        peer = lax.rem(tile + i, n_tile)
        deliver(peer, peer).wait_recv()
        return carry

    lax.fori_loop(1, n_tile, arrive, 0)

    def edge(side, target):
        return pltpu.make_async_remote_copy(
            src_ref=landed.at[:, 0 if side == 0 else WSIDE - 1],
            dst_ref=high if side == 0 else low,
            send_sem=halo_send.at[side],
            recv_sem=halo_recv.at[side],
            device_id=strip_id(target),
            device_id_type=mesh_id,
        )

    has_below = strip > 0
    has_above = strip < n_tile * n_band - 1

    @pl.when(has_below)
    def _():
        edge(0, strip - 1).start()

    @pl.when(has_above)
    def _():
        edge(1, strip + 1).start()

    grid_ref[...] = landed[...]

    def left(i, carry):
        peer = lax.rem(tile + i, n_tile)
        deliver(peer, peer).wait_send()
        return carry

    lax.fori_loop(1, n_tile, left, 0)

    def swapped(j, carry):
        swap(j).wait_send()
        return carry

    lax.fori_loop(0, blocks, swapped, 0)

    @pl.when(has_below)
    def _():
        edge(0, strip - 1).wait_send()
        edge(1, strip - 1).wait_recv()
        low_ref[...] = low[...]

    @pl.when(has_above)
    def _():
        edge(1, strip + 1).wait_send()
        edge(0, strip + 1).wait_recv()
        high_ref[...] = high[...]

    @pl.when(strip == 0)
    def _():
        low_ref[...] = jnp.zeros_like(low_ref)

    @pl.when(strip == n_tile * n_band - 1)
    def _():
        high_ref[...] = jnp.zeros_like(high_ref)


def pool_exchange(pooled, n_tile, n_band):
    cells, width = pooled.shape
    cells = WSIDE * CB
    per = math.gcd(n_tile, 4)
    blocks = n_tile // per
    half = jnp.bfloat16
    vmem = pl.BlockSpec(memory_space=pltpu.VMEM)
    return pl.pallas_call(
        functools.partial(pool_kernel, n_tile, n_band),
        in_specs=[vmem],
        out_specs=[vmem] * 3,
        out_shape=[
            jax.ShapeDtypeStruct((n_tile, WSIDE, CB, width), half),
            jax.ShapeDtypeStruct((n_tile, CB, width), half),
            jax.ShapeDtypeStruct((n_tile, CB, width), half),
        ],
        scratch_shapes=[
            pltpu.VMEM((blocks, per, cells, width), half),
            pltpu.VMEM((n_tile, WSIDE, CB, width), half),
            pltpu.VMEM((n_tile, WSIDE, CB, width), half),
            pltpu.VMEM((n_tile, CB, width), half),
            pltpu.VMEM((n_tile, CB, width), half),
            pltpu.SemaphoreType.DMA((blocks,)),
            pltpu.SemaphoreType.DMA((blocks,)),
            pltpu.SemaphoreType.DMA((n_tile,)),
            pltpu.SemaphoreType.DMA((n_tile,)),
            pltpu.SemaphoreType.DMA((2,)),
            pltpu.SemaphoreType.DMA((2,)),
        ],
        compiler_params=pltpu.CompilerParams(collective_id=0, has_side_effects=True),
        name="pool_exchange",
    )(pooled.reshape(n_tile, n_band, cells, width))


def bev_kernel(
    grid_ref,
    low_ref,
    high_ref,
    tap_ref,
    qkv_ref,
    out_ref,
    up_ref,
    down_ref,
    result_ref,
    wide,
    qv_s,
    out_s,
    up_s,
    down_s,
):
    step = pl.program_id(0)
    n_tile, _, _, width = grid_ref.shape
    span = result_ref.shape[1]

    @pl.when(step == 0)
    def _():
        turn_weights(qkv_ref, out_ref, up_ref, down_ref, qv_s, out_s, up_s, down_s)
        edge = jnp.zeros((WSIDE + 2, CB, width), jnp.float32)
        wide[:, :CB, :] = edge
        wide[:, (n_tile + 1) * CB :, :] = edge

        def fill(t, carry):
            to = pl.ds(pl.multiple_of((t + 1) * CB, CB), CB)
            wide[0, to, :] = low_ref[t].astype(jnp.float32)
            wide[WSIDE + 1, to, :] = high_ref[t].astype(jnp.float32)
            wide[1 : WSIDE + 1, to, :] = grid_ref[t].astype(jnp.float32)
            return carry

        lax.fori_loop(0, n_tile, fill, 0)

    at = pl.multiple_of(step * span, span)
    sums = [jnp.zeros((span, width), jnp.float32) for _ in range(WSIDE)]
    centers = []
    for r in range(WSIDE + 2):
        slab = wide[r, pl.ds(at, span + 2 * CB), :]
        for c in range(3):
            moved = slab[CB + c - 1 : CB + c - 1 + span]
            if c == 1:
                centers.append(moved)
            for row_tap in range(3):
                to = r - row_tap
                if 0 <= to < WSIDE:
                    tap = tap_ref[3 * row_tap + c : 3 * row_tap + c + 1, :]
                    sums[to] = sums[to] + moved * tap
    shaped = [centers[r + 1] + sums[r] for r in range(WSIDE)]
    count = span // CB
    x = jnp.concatenate(
        [shaped[r][w * CB : (w + 1) * CB] for w in range(count) for r in range(WSIDE)], axis=0
    ).astype(jnp.bfloat16)
    result = attend_columns(
        x, qv_s[...], qkv_ref[:, width : 2 * width], out_s[...], up_s[...], down_s[...]
    ).T
    for r in range(WSIDE):
        result_ref[r] = jnp.concatenate(
            [result[(w * WSIDE + r) * CB : (w * WSIDE + r + 1) * CB] for w in range(count)], axis=0
        ).astype(jnp.bfloat16)


def bev_block(grid, low, high, taps, weights):
    n_tile, _, _, width = grid.shape
    cols = n_tile * CB
    span = min(64, cols)
    inputs = (grid, low, high, taps, *weights)
    return pl.pallas_call(
        bev_kernel,
        grid=(cols // span,),
        in_specs=[whole(a) for a in inputs],
        out_specs=pl.BlockSpec((WSIDE, span, width), lambda i: (0, i, 0)),
        out_shape=jax.ShapeDtypeStruct((WSIDE, cols, width), jnp.bfloat16),
        scratch_shapes=[pltpu.VMEM((WSIDE + 2, cols + 2 * CB, width), jnp.float32)]
        + turned_scratch(*weights),
        name="bev_block",
    )(*inputs)


def shards(
    voxel_feat,
    window_count,
    voxel_cell,
    w_qkv_voxel,
    w_out_voxel,
    w_up_voxel,
    w_down_voxel,
    conv_taps,
    w_qkv_bev,
    w_out_bev,
    w_up_bev,
    w_down_bev,
):
    n_tile = lax.axis_size("tile")
    n_band = lax.axis_size("band")
    pooled = voxel_pool(
        voxel_feat,
        window_count,
        voxel_cell,
        (w_qkv_voxel, w_out_voxel, w_up_voxel, w_down_voxel),
        WSIDE * CB * n_tile * n_band,
    )
    grid, low, high = pool_exchange(pooled, n_tile, n_band)
    return bev_block(
        grid, low, high, conv_taps, (w_qkv_bev, w_out_bev, w_up_bev, w_down_bev)
    )


def solution(mesh):
    placed = (
        P(("tile", "band"), None, None),
        P(("tile", "band")),
        P(("tile", "band"), None),
        P(),
        P(),
        P(),
        P(),
        P(),
        P(),
        P(),
        P(),
        P(),
    )
    return jax.shard_map(
        shards,
        mesh=mesh,
        in_specs=placed,
        out_specs=P(("tile", "band"), None, None),
        check_vma=False,
    )
```
